128 devices in a mesh: blk: 64 (over z, x, y_lo, core), rep: 2 (over y_hi).
Axes of the slice: x: 4, y: 4 (y_hi: 2, y_lo: 2; y = y_hi * 2 + y_lo), z: 4, core: 2. Of those that a mesh axis runs over, the one named last changes fastest.
Arguments:
- tokens: int32 [32768, 69], P('blk'), may hold values from 0 to 63
- lengths: int32 [32768], P('blk'), may hold values from 16 to 69
- embed: bfloat16 [64, 256], replicated, may hold values from -6 to 6
- conv_w: bfloat16 [7, 32, 256], replicated, may hold values from -0.375 to 0.375
- conv_b: float32 [256], replicated, may hold values from -3 to 3
- inv_len: float32 [256], replicated, may hold values from 0.05 to 0.3
- hyper: float32 [2], replicated, may hold values from 0.5 to 2
- probes: bfloat16 [32768, 64], P('blk'), may hold values from -6 to 6
- prev_probes: bfloat16 [32768, 64], P(('blk', 'rep')), may hold values from -6 to 6
- coupling: float32 [64, 64], replicated, may hold values from -12 to 12
Outputs:
- block_a: float32 [64, 64], replicated
- block_r: float32 [64, 64], replicated
- next_probes: float32 [32768, 64], P(('blk', 'rep'))
The draws below stay inside these ranges and needn't reach their ends.
All inputs are finite; a program needn't handle non-finite values.
Results may differ from the reference program's by a relative error of at most 0.0065.
Values may be sent and summed in bfloat16 or wider, within the bound.
No kernel may reach another device: no remote copies, remote signals or barrier semaphores. Data moves between devices by JAX's collectives and lax.ppermute only.
A program may use at most 128 MiB of HBM per device.

```python
import math
import jax
import jax.numpy as jnp
import numpy as np
from jax import lax

CH = 256
KW = 7
SEQ = 69
VOCAB = 64
PROBES = 64
NS = 32768
GSIZE = 32
TOUT = 32


def set_ends(result, key, least, largest):
    shape = result.shape
    spot = [jax.random.randint(jax.random.fold_in(key, axis), (), 0, shape[axis]) for axis in range(len(shape))]
    result = result.at[tuple(spot)].set(least)
    longest = shape.index(max(shape))
    spot[longest] = (spot[longest] + 1) % shape[longest]
    return result.at[tuple(spot)].set(largest)


def block_scale(key, shape, shards, least, largest):
    gain, own = 1.0, jax.random.fold_in(key, 6)
    for axis_at, parts in shards:
        steps = jnp.exp(jax.random.uniform(jax.random.fold_in(own, axis_at), (parts,), jnp.float32, least / len(shards), largest / len(shards)))
        gain = gain * jnp.repeat(steps, shape[axis_at] // parts).reshape([-1 if axis == axis_at else 1 for axis in range(len(shape))])
    return gain


def rank_bounds(number_of, lean):
    weights = [(1 << 20) // math.isqrt(standing ** lean) + 1 for standing in range(1, number_of + 1)]
    scale = 1 + sum(weights) // (1 << 30)
    return np.cumsum(np.array([max(1, weight // scale) for weight in weights]))


def ranked(key, extent, amount, slope):
    listing = rank_bounds(amount, slope)
    lot = jax.random.randint(jax.random.fold_in(key, 1), extent, 0, int(listing[amount - 1]))
    rank = jnp.searchsorted(jnp.asarray(listing, jnp.int32), lot, side="right")
    return jax.random.permutation(jax.random.fold_in(key, 2), amount)[rank].astype(jnp.int32)


def bell_draw(stream_key, dims, scale, bound, cuts=(), kind=jnp.bfloat16):
    gain = block_scale(stream_key, dims, cuts, -0.22, 0.18) if cuts else 1.0
    entries = jax.random.normal(stream_key, dims, jnp.float32) * scale * gain
    return jnp.minimum(jnp.maximum(entries, -bound), bound).astype(kind)


def setup_inputs(seed: int = 0) -> dict:
    seeds = jax.random.split(jax.random.key(seed), 11)
    return {
        "tokens": set_ends(ranked(seeds[0], (NS, SEQ), VOCAB, 2), jax.random.fold_in(seeds[0], 3), 0, VOCAB - 1).astype(jnp.int32),
        "lengths": set_ends(jax.random.randint(seeds[1], (NS,), 16, SEQ + 1), jax.random.fold_in(seeds[1], 1), 16, SEQ).astype(jnp.int32),
        "embed": bell_draw(seeds[2], (VOCAB, CH), 1.0, 6.0),
        "conv_w": bell_draw(seeds[3], (KW, GSIZE, CH), (KW * GSIZE) ** -0.5, 0.375),
        "conv_b": bell_draw(seeds[4], (CH,), 0.5, 3.0, (), jnp.float32),
        "inv_len": jnp.clip(jnp.exp(jax.random.uniform(seeds[5], (CH,), jnp.float32, math.log(0.05), math.log(0.3))), 0.05, 0.3),
        "hyper": jnp.clip(jax.random.uniform(seeds[6], (2,), jnp.float32, 0.5, 2.0), 0.5, 2.0),
        "probes": bell_draw(seeds[7], (NS, PROBES), 1.0, 6.0, ((0, 64),)),
        "prev_probes": bell_draw(seeds[8], (NS, PROBES), 1.0, 6.0, ((0, 128),)),
        "coupling": bell_draw(seeds[9], (PROBES, PROBES), 2.0, 12.0, (), jnp.float32),
    }


def upper_factor(gram):
    order = gram.shape[0]
    index_row = jnp.arange(order, dtype=jnp.int32)

    def column_step(column, carry):
        work, lower = carry
        pivot = lax.dynamic_slice(work, (column, column), (1, 1))[0, 0]
        vector = lax.dynamic_slice_in_dim(work, column, 1, 1)[:, 0]
        vector = jnp.where(index_row >= column, vector * lax.rsqrt(pivot), 0.0)
        lower = lower + vector[:, None] * (index_row == column).astype(jnp.float32)[None, :]
        work = work - vector[:, None] * vector[None, :]
        return (work, lower)
    _, lower = lax.fori_loop(0, order, column_step, (gram, jnp.zeros_like(gram)))
    return lower.T

def upper_inverse(upper):
    order = upper.shape[0]
    index_row = jnp.arange(order, dtype=jnp.int32)

    def row_step(count, solved):
        row = order - 1 - count
        upper_row = lax.dynamic_slice_in_dim(upper, row, 1, 0)
        diag_value = lax.dynamic_slice(upper, (row, row), (1, 1))[0, 0]
        unit_row = (index_row == row).astype(jnp.float32)[None, :]
        product = jnp.dot(upper_row, solved, precision=lax.Precision.HIGHEST, preferred_element_type=jnp.float32)
        new_row = (unit_row - product) / diag_value
        return solved + (index_row == row).astype(jnp.float32)[:, None] * new_row
    return lax.fori_loop(0, order, row_step, jnp.zeros_like(upper))

def features_block(tok_block, len_block, embed, conv_w, conv_b, inv_len):
    block_rows = tok_block.shape[0]
    group_count = CH // GSIZE
    embedded = jnp.take(embed, tok_block, axis=0).astype(jnp.float32)
    running = jnp.zeros((block_rows, TOUT, group_count, GSIZE), jnp.float32)
    for tap_index in range(KW):
        window = lax.slice(embedded, (0, tap_index, 0), (block_rows, tap_index + 2 * (TOUT - 1) + 1, CH), (1, 2, 1))
        window = window.reshape(block_rows, TOUT, group_count, GSIZE)
        kernel_tap = conv_w[tap_index].astype(jnp.float32).reshape(GSIZE, group_count, GSIZE)
        running = running + jnp.einsum('btgi,igo->btgo', window, kernel_tap, preferred_element_type=jnp.float32)
    preact = running.reshape(block_rows, TOUT, CH) + conv_b
    counts = (len_block - KW) // 2 + 1
    valid_mask = (jnp.arange(TOUT, dtype=jnp.int32)[None, :] < counts[:, None]).astype(jnp.float32)
    activated = jax.nn.gelu(preact, approximate=True) * valid_mask[:, :, None]
    pooled = lax.optimization_barrier(jnp.sum(activated, axis=1)) / counts.astype(jnp.float32)[:, None]
    row_mean = lax.optimization_barrier(jnp.mean(pooled, axis=1, keepdims=True))
    centered = pooled - row_mean
    row_var = lax.optimization_barrier(jnp.mean(centered * centered, axis=1, keepdims=True))
    normed = centered * lax.rsqrt(row_var + 1e-05)
    return (normed * inv_len).astype(jnp.bfloat16)

def reference(tokens, lengths, embed, conv_w, conv_b, inv_len, hyper, probes, prev_probes, coupling):
    block_rows = math.gcd(NS, 256)
    block_count = NS // block_rows

    def feature_step(pair):
        return features_block(pair[0], pair[1], embed, conv_w, conv_b, inv_len)
    feat = lax.map(feature_step, (tokens.reshape(block_count, block_rows, SEQ), lengths.reshape(block_count, block_rows)))
    feat = feat.reshape(NS, CH)
    feat_wide = lax.optimization_barrier(feat).astype(jnp.float32)
    sq_all = lax.optimization_barrier(jnp.sum(feat_wide * feat_wide, axis=1))
    probes_wide = probes.astype(jnp.float32)
    amplitude = hyper[0]
    noise_var = hyper[1]
    kern_rows = math.gcd(NS, 512)
    kern_count = NS // kern_rows

    def kernel_rows(pair):
        rows_feat, rows_sq = pair
        inner_prod = jnp.dot(rows_feat, feat_wide.T, preferred_element_type=jnp.float32)
        distance = jnp.maximum(rows_sq[:, None] + sq_all[None, :] - 2.0 * inner_prod, 0.0)
        weights = (amplitude * jnp.exp(-0.5 * distance)).astype(jnp.bfloat16)
        weights = lax.optimization_barrier(weights).astype(jnp.float32)
        return jnp.dot(weights, probes_wide, preferred_element_type=jnp.float32)
    applied = lax.map(kernel_rows, (feat_wide.reshape(kern_count, kern_rows, CH), sq_all.reshape(kern_count, kern_rows)))
    applied = applied.reshape(NS, PROBES) + noise_var * probes_wide
    inv_root = 1.0 / math.sqrt(NS)
    basis = probes_wide * inv_root
    coupled = jnp.dot(prev_probes.astype(jnp.float32), coupling.T, precision=lax.Precision.HIGHEST, preferred_element_type=jnp.float32) * inv_root
    image = applied * inv_root - coupled
    block_a = jnp.dot(basis.T, image, precision=lax.Precision.HIGHEST, preferred_element_type=jnp.float32)
    resid = image - jnp.dot(basis, block_a, precision=lax.Precision.HIGHEST, preferred_element_type=jnp.float32)
    gram = jnp.dot(resid.T, resid, precision=lax.Precision.HIGHEST, preferred_element_type=jnp.float32)
    upper = upper_factor(gram)
    inverse = upper_inverse(upper)
    next_probes = jnp.dot(resid, inverse, precision=lax.Precision.HIGHEST, preferred_element_type=jnp.float32) * math.sqrt(NS)
    return (block_a, upper, next_probes)
```

```python
import functools
import math

import jax
import jax.numpy as jnp
from jax import lax
from jax.experimental import pallas as pl
from jax.experimental.pallas import tpu as pltpu
from jax.sharding import PartitionSpec as P

LOG2E = math.log2(math.e)
HIGHEST = lax.Precision.HIGHEST
AXES = ("blk", "rep")
RING = 4


def coords_of(index):
    rep, blk = index % 2, index // 2
    return blk // 16, (blk // 4) % 4, rep * 2 + (blk // 2) % 2, blk % 2


def index_of(z, x, y, core):
    return (((z * 4 + x) * 2 + y % 2) * 2 + core) * 2 + y // 2


def moved(move):
    return [(i, index_of(*move(*coords_of(i)))) for i in range(128)]


def core_swap():
    return moved(lambda z, x, y, c: (z, x, y, 1 - c))


def shift_y(step):
    return moved(lambda z, x, y, c: (z, x, (y + step) % RING, c))


def shift_z(step):
    return moved(lambda z, x, y, c: ((z + step) % RING, x, y, c))


def shift_x(step):
    return moved(lambda z, x, y, c: (z, (x + step) % RING, y, c))


def shift_by_core(step, core_of_z):
    def move(z, x, y, c):
        if c == core_of_z:
            return (z + step) % RING, x, y, c
        return z, (x + step) % RING, y, c

    return moved(move)


def send(value, perm):
    return lax.ppermute(value, AXES, perm)


def dot(left, right, dims, precision=None):
    return lax.dot_general(
        left, right, (dims, ((), ())), precision=precision, preferred_element_type=jnp.float32
    )


NN = ((1,), (0,))
NT = ((1,), (1,))
TN = ((0,), (0,))


def conv_kernel(
    taps, half_ref, tok_ref, len_ref, embed_ref, w_ref, bias_ref, inv_len_ref, probe_ref,
    cols_ref, rows_ref, table_ref, left_ref, onehot_ref, acc_ref,
):
    vocab, channels = embed_ref.shape
    width = w_ref.shape[1]
    seq, samples = tok_ref.shape
    outputs = (seq - taps) // 2 + 1
    depth = taps * vocab
    group_in = lax.broadcasted_iota(jnp.int32, (channels, channels), 0) // width
    group_out = lax.broadcasted_iota(jnp.int32, (channels, channels), 1) // width
    same = group_in == group_out
    embed = embed_ref[...]
    table_ref[...] = jnp.zeros_like(table_ref)
    for k in range(taps):
        tiled = jnp.concatenate([w_ref[k].astype(jnp.float32)] * (channels // width), axis=0)
        dense = jnp.where(same, tiled, 0.0).astype(jnp.bfloat16)
        entry = dot(embed, dense, NN)
        if k == 0:
            entry = entry + bias_ref[...]
        table_ref[k * vocab : (k + 1) * vocab, :] = entry
    table = table_ref[...].T
    high = table.astype(jnp.bfloat16)
    left_ref[:channels, :] = high
    left_ref[channels:, :] = (table - high.astype(jnp.float32)).astype(jnp.bfloat16)

    vocab_ids = lax.broadcasted_iota(jnp.int32, (vocab, samples), 0)

    def spread(s, carry):
        hit = tok_ref[pl.ds(s, 1), :] == vocab_ids
        onehot_ref[pl.ds(pl.multiple_of(s * vocab, vocab), vocab), :] = jnp.where(
            hit, 1.0, 0.0
        ).astype(jnp.bfloat16)
        return carry

    lax.fori_loop(0, seq, spread, 0, unroll=3)

    counts = (len_ref[...] - taps) // 2 + 1
    acc_ref[...] = jnp.zeros_like(acc_ref)
    root = math.sqrt(2.0 / math.pi)

    def position(t):
        start = pl.multiple_of(t * 2 * vocab, 2 * vocab)
        window = onehot_ref[pl.ds(start, depth), :]
        both = dot(left_ref[:, :depth], window, NN)
        pre = both[:channels] + both[channels:]
        inner = pre * (root + (root * 0.044715) * (pre * pre))
        active = pre + pre * jnp.tanh(inner)
        return jnp.where(t < counts, active, 0.0)

    def positions(step, carry):
        total = position(step * 2) + position(step * 2 + 1)
        acc_ref[...] += total
        return carry

    lax.fori_loop(0, outputs // 2, positions, 0)

    pooled = acc_ref[...] * (0.5 / counts.astype(jnp.float32))
    centered = pooled - jnp.mean(pooled, axis=0, keepdims=True)
    spread_sq = jnp.mean(centered * centered, axis=0, keepdims=True)
    normed = centered * lax.rsqrt(spread_sq + 1e-05)
    feat = (normed.T * inv_len_ref[...]).astype(jnp.bfloat16)
    cols_ref[:samples, :] = feat
    cols_ref[samples:, :] = probe_ref[...]
    rows_ref[...] = feat.astype(jnp.float32).T.astype(jnp.bfloat16)


def conv_features(tok_t, lengths, embed, conv_w, conv_b, inv_len, probes_t, half):
    seq, rows = tok_t.shape
    vocab, channels = embed.shape
    taps = conv_w.shape[0]
    samples = rows // 2
    width = probes_t.shape[0]
    depth = -(-taps * vocab // 128) * 128
    whole = lambda shape: pl.BlockSpec(shape, lambda i, h: (0,) * len(shape))
    part = lambda lead: pl.BlockSpec((lead, samples), lambda i, h: (0, h[0]))
    return pl.pallas_call(
        functools.partial(conv_kernel, taps),
        grid_spec=pltpu.PrefetchScalarGridSpec(
            num_scalar_prefetch=1,
            grid=(1,),
            in_specs=[
                part(seq),
                part(1),
                whole((vocab, channels)),
                whole(conv_w.shape),
                whole((1, channels)),
                whole((1, channels)),
                part(width),
            ],
            out_specs=[whole((samples + width, channels)), whole((channels, samples))],
            scratch_shapes=[
                pltpu.VMEM((depth, channels), jnp.float32),
                pltpu.VMEM((2 * channels, depth), jnp.bfloat16),
                pltpu.VMEM((seq * vocab, samples), jnp.bfloat16),
                pltpu.VMEM((channels, samples), jnp.float32),
            ],
        ),
        out_shape=[
            jax.ShapeDtypeStruct((samples + width, channels), jnp.bfloat16),
            jax.ShapeDtypeStruct((channels, samples), jnp.bfloat16),
        ],
        name="conv_features",
    )(
        half, tok_t, lengths.reshape(1, rows), embed, conv_w,
        conv_b.reshape(1, channels), inv_len.reshape(1, channels), probes_t,
    )


def apply_kernel(row_count, col_count, resume, hyper_ref, *refs):
    row_refs = refs[:row_count]
    col_refs = refs[row_count : row_count + col_count]
    rest = refs[row_count + col_count :]
    start_refs, out_refs, (half_ref,) = rest[: 2 * resume], rest[2 * resume : -1], rest[-1:]
    channels, samples = row_refs[0].shape
    half_rows = row_count // 2
    top = jnp.log2(jnp.full((1, 128), hyper_ref[0], jnp.float32))[:, :1]
    for i, row_ref in enumerate(row_refs):
        wide = row_ref[...].astype(jnp.float32)
        half_ref[i : i + 1, :] = (0.5 * LOG2E) * jnp.sum(wide * wide, axis=0, keepdims=True)
    for side in range(2):
        if resume:
            out_refs[side][...] = start_refs[side][...]
        else:
            out_refs[side][...] = jnp.zeros_like(out_refs[side])

    def block(col):
        feat = col[:samples, :]
        probes = col[samples:, :]
        wide = feat.astype(jnp.float32)
        bias = (0.5 * LOG2E) * jnp.sum(wide * wide, axis=1, keepdims=True) - top
        bias = jnp.broadcast_to(bias, (samples, samples))
        for i, row_ref in enumerate(row_refs):
            inner = dot(feat, row_ref[...], NN)
            power = jnp.minimum(inner * LOG2E - bias - half_ref[i : i + 1, :], top)
            weights = jnp.exp2(power).astype(jnp.bfloat16)
            out_refs[i // half_rows][i % half_rows] += dot(probes, weights, NN)

    for col_ref in col_refs:
        if len(col_ref.shape) == 2:
            block(col_ref[...])
        else:

            def step(j, carry, col_ref=col_ref):
                block(col_ref[j])
                return carry

            lax.fori_loop(0, col_ref.shape[0], step, 0)


def apply_rows(hyper, rows, cols, start=()):
    samples = rows[0].shape[1]
    width = cols[0].shape[-2] - samples
    half_rows = len(rows) // 2
    vmem = pl.BlockSpec(memory_space=pltpu.VMEM)
    blocks = sum(math.prod(c.shape[:-2]) for c in cols)
    pairs = blocks * len(rows) * samples * samples
    out = jax.ShapeDtypeStruct((half_rows, width, samples), jnp.float32)
    return pl.pallas_call(
        functools.partial(apply_kernel, len(rows), len(cols), 1 if start else 0),
        out_shape=[out, out],
        in_specs=[pl.BlockSpec(memory_space=pltpu.SMEM)]
        + [vmem] * (len(rows) + len(cols) + len(start)),
        out_specs=[vmem, vmem],
        scratch_shapes=[pltpu.VMEM((len(rows), samples), jnp.float32)],
        cost_estimate=pl.CostEstimate(
            flops=2 * pairs * (256 + 64), transcendentals=pairs, bytes_accessed=4 << 20
        ),
        name="apply_rows",
    )(hyper, *rows, *cols, *start)


def gram_kernel(
    inv_root, hyper_ref, own_ref, one_ref, two_ref, three_ref, half_ref, probe_ref, prev_ref,
    coupling_ref, image_ref, packed_ref,
):
    del half_ref
    probes = probe_ref[...].astype(jnp.float32)
    coupled = dot(coupling_ref[...], prev_ref[...].astype(jnp.float32), NN, HIGHEST) * inv_root
    applied = (own_ref[...] + two_ref[...]) + (one_ref[...] + three_ref[...])
    applied = applied + hyper_ref[1] * probes
    image = applied * inv_root - coupled
    basis = probes * inv_root
    image_ref[...] = image
    size = image.shape[0]
    packed_ref[:size, :size] = dot(basis, image, NT, HIGHEST)
    packed_ref[:size, size:] = dot(image, image, NT, HIGHEST)
    square = dot(basis, basis, NT, HIGHEST)
    packed_ref[size:, :size] = square[: size // 2]
    packed_ref[size:, size:] = square[size // 2 :]


def gram_stage(inv_root, hyper, parts, probes_t, prev_t, coupling, half):
    size, samples = parts[0].shape
    whole = lambda shape: pl.BlockSpec(shape, lambda i, h: (0,) * len(shape))

    def kernel(half_ref, hyper_ref, own, one, two, three, probe, prev, coup, image, packed):
        gram_kernel(
            inv_root, hyper_ref, own, one, two, three, half_ref, probe, prev, coup, image, packed
        )

    return pl.pallas_call(
        kernel,
        grid_spec=pltpu.PrefetchScalarGridSpec(
            num_scalar_prefetch=1,
            grid=(1,),
            in_specs=[pl.BlockSpec(memory_space=pltpu.SMEM)]
            + [whole((size, samples))] * 4
            + [
                pl.BlockSpec((size, samples), lambda i, h: (0, h[0])),
                whole((size, samples)),
                whole((size, size)),
            ],
            out_specs=[whole((size, samples)), whole((size * 3 // 2, 2 * size))],
        ),
        out_shape=[
            jax.ShapeDtypeStruct((size, samples), jnp.float32),
            jax.ShapeDtypeStruct((size * 3 // 2, 2 * size), jnp.float32),
        ],
        name="gram_stage",
    )(half, hyper, *parts, probes_t, prev_t, coupling)


def finish_kernel(inv_root, half_ref, packed_ref, image_ref, probe_ref, a_ref, r_ref, next_ref):
    size = image_ref.shape[0]
    block_a = packed_ref[:size, :size]
    image_sq = packed_ref[:size, size:]
    square = jnp.concatenate([packed_ref[size:, :size], packed_ref[size:, size:]], axis=0)
    twice = 2.0 * block_a - dot(square, block_a, NN, HIGHEST)
    gram = image_sq - dot(block_a, twice, TN, HIGHEST)
    basis = probe_ref[...].astype(jnp.float32) * inv_root
    resid = image_ref[...] - dot(block_a, basis, TN, HIGHEST)

    row_id = lax.broadcasted_iota(jnp.int32, (size, 2 * size), 0)
    lane_id = lax.broadcasted_iota(jnp.int32, (size, 2 * size), 1)
    unit = jnp.where(lane_id == row_id + size, 1.0, 0.0)
    work = jnp.concatenate([gram, jnp.zeros_like(gram)], axis=1) + unit
    tiles = [work[8 * i : 8 * i + 8, :] for i in range(size // 8)]
    sub_id = lax.broadcasted_iota(jnp.int32, (8, 2 * size), 0)
    for j in range(size):
        home, place = divmod(j, 8)
        row = jnp.broadcast_to(tiles[home][place : place + 1, :], (8, 2 * size))
        scale = lax.rsqrt(jnp.broadcast_to(row[:, j : j + 1], (8, 2 * size)))
        row = row * scale
        for i in range(home, size // 8):
            column = jnp.broadcast_to(tiles[i][:, j : j + 1], (8, 2 * size)) * scale
            if i == home:
                column = jnp.where(sub_id > place, column, 0.0)
            tiles[i] = tiles[i] - column * row
            if i == home:
                tiles[i] = jnp.where(sub_id == place, row, tiles[i])
    work = jnp.concatenate(tiles, axis=0)
    upper_rows = lax.broadcasted_iota(jnp.int32, (size, size), 0)
    upper_cols = lax.broadcasted_iota(jnp.int32, (size, size), 1)
    a_ref[...] = block_a
    r_ref[...] = jnp.where(upper_cols >= upper_rows, work[:, :size], 0.0)
    next_ref[...] = dot(work[:, size:], resid, NN, HIGHEST) * (1.0 / inv_root)


def finish(inv_root, packed, image, probes_t, half):
    size, samples = image.shape
    whole = lambda shape: pl.BlockSpec(shape, lambda i, h: (0,) * len(shape))
    return pl.pallas_call(
        functools.partial(finish_kernel, inv_root),
        grid_spec=pltpu.PrefetchScalarGridSpec(
            num_scalar_prefetch=1,
            grid=(1,),
            in_specs=[
                whole(packed.shape),
                whole(image.shape),
                pl.BlockSpec((size, samples), lambda i, h: (0, h[0])),
            ],
            out_specs=[whole((size, size)), whole((size, size)), whole((size, samples))],
        ),
        out_shape=[
            jax.ShapeDtypeStruct((size, size), jnp.float32),
            jax.ShapeDtypeStruct((size, size), jnp.float32),
            jax.ShapeDtypeStruct((size, samples), jnp.float32),
        ],
        name="finish",
    )(half, packed, image, probes_t)


def ring_sum(value, shift):
    one, two, three = (send(value, shift(s)) for s in (1, 2, 3))
    return (value + two) + (one + three)


def per_device(
    tokens, lengths, embed, conv_w, conv_b, inv_len, hyper, probes, prev_probes, coupling
):
    total_rows = tokens.shape[0] * lax.axis_size("blk")
    inv_root = 1.0 / math.sqrt(total_rows)
    half = lax.axis_index("rep").astype(jnp.int32).reshape(1)
    probes_t = probes.T
    cols, rows = conv_features(
        tokens.T, lengths, embed, conv_w, conv_b, inv_len, probes_t, half
    )
    near = [send(cols, shift_by_core(s, 0)) for s in (1, 2, 3)]
    own_rows = [rows] + [send(rows, shift_y(s)) for s in (1, 2, 3)]
    group = jnp.stack([cols] + near)
    far = [send(group, shift_by_core(s, 1)) for s in (1, 3, 2)]
    other_rows = [send(r, core_swap()) for r in own_rows]
    all_rows = own_rows + other_rows
    partial = apply_rows(hyper, all_rows, [group])
    for block in far:
        partial = apply_rows(hyper, all_rows, [block], partial)
    own, other = partial
    joint = own + send(other, core_swap())
    parts = [joint[0]] + [send(joint[s], shift_y(-s)) for s in (1, 2, 3)]
    image, packed = gram_stage(inv_root, hyper, parts, probes_t, prev_probes.T, coupling, half)
    packed = packed + send(packed, core_swap())
    for shift in (shift_z, shift_x, shift_y):
        packed = ring_sum(packed, shift)
    block_a, upper, next_t = finish(inv_root, packed, image, probes_t, half)
    return (block_a, upper, next_t.T)


def solution(mesh):
    return jax.shard_map(
        per_device,
        mesh=mesh,
        in_specs=(
            P("blk", None),
            P("blk"),
            P(),
            P(),
            P(),
            P(),
            P(),
            P("blk", None),
            P(("blk", "rep"), None),
            P(),
        ),
        out_specs=(P(), P(), P(("blk", "rep"), None)),
        check_vma=False,
    )
```

```python
import functools
import math

import jax
import jax.numpy as jnp
from jax import lax
from jax.experimental import pallas as pl
from jax.experimental.pallas import tpu as pltpu
from jax.sharding import PartitionSpec as P


LOG2E = math.log2(math.e)
HIGHEST = lax.Precision.HIGHEST
AXES = ("blk", "rep")
RING = 4


def coords_of(index):
    rep, blk = index % 2, index // 2
    return blk // 16, (blk // 4) % 4, rep * 2 + (blk // 2) % 2, blk % 2


def index_of(z, x, y, core):
    return (((z * 4 + x) * 2 + y % 2) * 2 + core) * 2 + y // 2


def moved(move):
    return [(i, index_of(*move(*coords_of(i)))) for i in range(128)]


def core_swap():
    return moved(lambda z, x, y, c: (z, x, y, 1 - c))


def shift_y(step):
    return moved(lambda z, x, y, c: (z, x, (y + step) % RING, c))


def shift_z(step):
    return moved(lambda z, x, y, c: ((z + step) % RING, x, y, c))


def shift_x(step):
    return moved(lambda z, x, y, c: (z, (x + step) % RING, y, c))


def shift_by_core(step, core_of_z):
    def move(z, x, y, c):
        if c == core_of_z:
            return (z + step) % RING, x, y, c
        return z, (x + step) % RING, y, c

    return moved(move)


def send(value, perm):
    return lax.ppermute(value, AXES, perm)


def dot(left, right, dims, precision=None):
    return lax.dot_general(
        left, right, (dims, ((), ())), precision=precision, preferred_element_type=jnp.float32
    )


NN = ((1,), (0,))
NT = ((1,), (1,))
TN = ((0,), (0,))


def conv_kernel(
    taps, half_ref, tok_ref, len_ref, embed_ref, w_ref, bias_ref, inv_len_ref, probe_ref,
    cols_ref, rows_ref, table_ref, left_ref, onehot_ref, acc_ref,
):
    vocab, channels = embed_ref.shape
    width = w_ref.shape[1]
    seq, samples = tok_ref.shape
    outputs = (seq - taps) // 2 + 1
    depth = taps * vocab
    group_in = lax.broadcasted_iota(jnp.int32, (channels, channels), 0) // width
    group_out = lax.broadcasted_iota(jnp.int32, (channels, channels), 1) // width
    same = group_in == group_out
    embed = embed_ref[...]
    table_ref[...] = jnp.zeros_like(table_ref)
    for k in range(taps):
        tiled = jnp.concatenate([w_ref[k].astype(jnp.float32)] * (channels // width), axis=0)
        dense = jnp.where(same, tiled, 0.0).astype(jnp.bfloat16)
        entry = dot(embed, dense, NN)
        if k == 0:
            entry = entry + bias_ref[...]
        table_ref[k * vocab : (k + 1) * vocab, :] = entry
    table = table_ref[...].T
    high = table.astype(jnp.bfloat16)
    left_ref[:channels, :] = high
    left_ref[channels:, :] = (table - high.astype(jnp.float32)).astype(jnp.bfloat16)

    vocab_ids = lax.broadcasted_iota(jnp.int32, (vocab, samples), 0)

    def spread(s, carry):
        hit = tok_ref[pl.ds(s, 1), :] == vocab_ids
        onehot_ref[pl.ds(pl.multiple_of(s * vocab, vocab), vocab), :] = jnp.where(
            hit, 1.0, 0.0
        ).astype(jnp.bfloat16)
        return carry

    lax.fori_loop(0, seq, spread, 0, unroll=3)

    counts = (len_ref[...] - taps) // 2 + 1
    acc_ref[...] = jnp.zeros_like(acc_ref)
    root = math.sqrt(2.0 / math.pi)

    def position(t):
        start = pl.multiple_of(t * 2 * vocab, 2 * vocab)
        window = onehot_ref[pl.ds(start, depth), :]
        both = dot(left_ref[:, :depth], window, NN)
        pre = both[:channels] + both[channels:]
        inner = pre * (root + (root * 0.044715) * (pre * pre))
        active = pre + pre * jnp.tanh(inner)
        return jnp.where(t < counts, active, 0.0)

    def positions(step, carry):
        total = position(step * 2) + position(step * 2 + 1)
        acc_ref[...] += total
        return carry

    lax.fori_loop(0, outputs // 2, positions, 0)

    pooled = acc_ref[...] * (0.5 / counts.astype(jnp.float32))
    centered = pooled - jnp.mean(pooled, axis=0, keepdims=True)
    spread_sq = jnp.mean(centered * centered, axis=0, keepdims=True)
    normed = centered * lax.rsqrt(spread_sq + 1e-05)
    feat = (normed.T * inv_len_ref[...]).astype(jnp.bfloat16)
    cols_ref[:samples, :] = feat
    cols_ref[samples:, :] = probe_ref[...]
    rows_ref[...] = feat.astype(jnp.float32).T.astype(jnp.bfloat16)


def conv_features(tok_t, lengths, embed, conv_w, conv_b, inv_len, probes_t, half):
    seq, rows = tok_t.shape
    vocab, channels = embed.shape
    taps = conv_w.shape[0]
    samples = rows // 2
    width = probes_t.shape[0]
    depth = -(-taps * vocab // 128) * 128
    whole = lambda shape: pl.BlockSpec(shape, lambda i, h: (0,) * len(shape))
    part = lambda lead: pl.BlockSpec((lead, samples), lambda i, h: (0, h[0]))
    return pl.pallas_call(
        functools.partial(conv_kernel, taps),
        grid_spec=pltpu.PrefetchScalarGridSpec(
            num_scalar_prefetch=1,
            grid=(1,),
            in_specs=[
                part(seq),
                part(1),
                whole((vocab, channels)),
                whole(conv_w.shape),
                whole((1, channels)),
                whole((1, channels)),
                part(width),
            ],
            out_specs=[whole((samples + width, channels)), whole((channels, samples))],
            scratch_shapes=[
                pltpu.VMEM((depth, channels), jnp.float32),
                pltpu.VMEM((2 * channels, depth), jnp.bfloat16),
                pltpu.VMEM((seq * vocab, samples), jnp.bfloat16),
                pltpu.VMEM((channels, samples), jnp.float32),
            ],
        ),
        out_shape=[
            jax.ShapeDtypeStruct((samples + width, channels), jnp.bfloat16),
            jax.ShapeDtypeStruct((channels, samples), jnp.bfloat16),
        ],
        name="conv_features",
    )(
        half, tok_t, lengths.reshape(1, rows), embed, conv_w,
        conv_b.reshape(1, channels), inv_len.reshape(1, channels), probes_t,
    )


def apply_kernel(row_count, col_count, resume, hyper_ref, *refs):
    rows = refs[:row_count]
    cols = refs[row_count : row_count + col_count]
    rest = refs[row_count + col_count :]
    start_refs, (out_ref, half_ref) = rest[:resume], rest[resume:]
    _, samples = rows[0].shape
    depth = cols[0].shape[0]
    top = jnp.log2(jnp.full((1, 128), hyper_ref[0], jnp.float32))[:, :1]
    if resume:
        out_ref[...] = start_refs[0][...]
    else:
        out_ref[...] = jnp.zeros_like(out_ref)
    for i in range(row_count):
        wide = rows[i][...].astype(jnp.float32)
        half_ref[i : i + 1, :] = (0.5 * LOG2E) * jnp.sum(wide * wide, axis=0, keepdims=True)
    for g in range(col_count):
        feat = jnp.concatenate([cols[g][d, :samples, :] for d in range(depth)], axis=0)
        probes = jnp.concatenate([cols[g][d, samples:, :] for d in range(depth)], axis=1)
        wide = feat.astype(jnp.float32)
        bias = (0.5 * LOG2E) * jnp.sum(wide * wide, axis=1, keepdims=True) - top
        bias = jnp.broadcast_to(bias, (depth * samples, samples))
        for i in range(row_count):
            inner = dot(feat, rows[i][...], NN)
            power = jnp.minimum(inner * LOG2E - bias - half_ref[i : i + 1, :], top)
            weights = jnp.exp2(power).astype(jnp.bfloat16)
            out_ref[i] += dot(probes, weights, NN)


def apply_rows(hyper, rows, cols, start=()):
    channels, samples = rows[0].shape
    depth, tall, _ = cols[0].shape
    width = tall - samples
    vmem = pl.BlockSpec(memory_space=pltpu.VMEM)
    pairs = len(cols) * depth * len(rows) * samples * samples
    return pl.pallas_call(
        functools.partial(apply_kernel, len(rows), len(cols), len(start)),
        out_shape=jax.ShapeDtypeStruct((len(rows), width, samples), jnp.float32),
        in_specs=[pl.BlockSpec(memory_space=pltpu.SMEM)]
        + [vmem] * (len(rows) + len(cols) + len(start)),
        out_specs=vmem,
        scratch_shapes=[pltpu.VMEM((len(rows), samples), jnp.float32)],
        compiler_params=pltpu.CompilerParams(vmem_limit_bytes=24 << 20),
        cost_estimate=pl.CostEstimate(
            flops=2 * pairs * (channels + width), transcendentals=pairs, bytes_accessed=4 << 20
        ),
        name="apply_rows",
    )(hyper, *rows, *cols, *start)


def gram_kernel(
    inv_root, hyper_ref, own_ref, one_ref, two_ref, three_ref, half_ref, probe_ref, prev_ref,
    coupling_ref, image_ref, packed_ref,
):
    del half_ref
    probes = probe_ref[...].astype(jnp.float32)
    coupled = dot(coupling_ref[...], prev_ref[...].astype(jnp.float32), NN, HIGHEST) * inv_root
    applied = (own_ref[...] + two_ref[...]) + (one_ref[...] + three_ref[...])
    applied = applied + hyper_ref[1] * probes
    image = applied * inv_root - coupled
    basis = probes * inv_root
    image_ref[...] = image
    size = image.shape[0]
    packed_ref[:size, :size] = dot(basis, image, NT, HIGHEST)
    image_sq = dot(image, image, NT, HIGHEST)
    basis_sq = dot(basis, basis, NT, HIGHEST)
    down = lax.broadcasted_iota(jnp.int32, (size, size), 0)
    across = lax.broadcasted_iota(jnp.int32, (size, size), 1)
    packed_ref[:size, size:] = jnp.where(across >= down, image_sq, basis_sq)
    diagonal = jnp.sum(jnp.where(across == down, basis_sq, 0.0), axis=0, keepdims=True)
    packed_ref[size:, :size] = jnp.broadcast_to(diagonal, (8, size))
    packed_ref[size:, size:] = jnp.zeros((8, size), jnp.float32)


def gram_stage(inv_root, hyper, parts, probes_t, prev_t, coupling, half):
    size, samples = parts[0].shape
    whole = lambda shape: pl.BlockSpec(shape, lambda i, h: (0,) * len(shape))

    def kernel(half_ref, hyper_ref, own, one, two, three, probe, prev, coup, image, packed):
        gram_kernel(
            inv_root, hyper_ref, own, one, two, three, half_ref, probe, prev, coup, image, packed
        )

    return pl.pallas_call(
        kernel,
        grid_spec=pltpu.PrefetchScalarGridSpec(
            num_scalar_prefetch=1,
            grid=(1,),
            in_specs=[pl.BlockSpec(memory_space=pltpu.SMEM)]
            + [whole((size, samples))] * 4
            + [
                pl.BlockSpec((size, samples), lambda i, h: (0, h[0])),
                whole((size, samples)),
                whole((size, size)),
            ],
            out_specs=[whole((size, samples)), whole((size + 8, 2 * size))],
        ),
        out_shape=[
            jax.ShapeDtypeStruct((size, samples), jnp.float32),
            jax.ShapeDtypeStruct((size + 8, 2 * size), jnp.float32),
        ],
        name="gram_stage",
    )(half, hyper, *parts, probes_t, prev_t, coupling)


PANEL = 4


def finish_kernel(inv_root, half_ref, packed_ref, image_ref, probe_ref, a_ref, r_ref, next_ref):
    size = image_ref.shape[0]
    block_a = packed_ref[:size, :size]
    mixed = packed_ref[:size, size:]
    mixed_t = mixed.T
    diagonal = packed_ref[size : size + 1, :size]
    down = lax.broadcasted_iota(jnp.int32, (size, size), 0)
    across = lax.broadcasted_iota(jnp.int32, (size, size), 1)
    image_sq = jnp.where(across >= down, mixed, mixed_t)
    square = jnp.where(across == down, diagonal, jnp.where(across < down, mixed, mixed_t))
    twice = 2.0 * block_a - dot(square, block_a, NN, HIGHEST)
    gram = image_sq - dot(block_a, twice, TN, HIGHEST)
    basis = probe_ref[...].astype(jnp.float32) * inv_root
    resid = image_ref[...] - dot(block_a, basis, TN, HIGHEST)

    unit = jnp.where(across == down, 1.0, 0.0)
    work = jnp.concatenate([gram, unit], axis=1)
    tiles = [work[8 * i : 8 * i + 8, :] for i in range(size // 8)]
    wide = (8, 2 * size)
    sub_id = lax.broadcasted_iota(jnp.int32, wide, 0)
    for j in range(0, size, PANEL):
        home, place = divmod(j, 8)
        rows = [
            jnp.broadcast_to(tiles[home][place + a : place + a + 1, :], wide)
            for a in range(PANEL)
        ]
        corner = [
            [jnp.broadcast_to(rows[a][:, j + b : j + b + 1], wide) if b >= a else None
             for b in range(PANEL)]
            for a in range(PANEL)
        ]
        scales = []
        for a in range(PANEL):
            scale = lax.rsqrt(corner[a][a])
            scales.append(scale)
            rows[a] = rows[a] * scale
            for b in range(a + 1, PANEL):
                corner[a][b] = corner[a][b] * scale
            for c in range(a + 1, PANEL):
                rows[c] = rows[c] - corner[a][c] * rows[a]
                for b in range(c, PANEL):
                    corner[c][b] = corner[c][b] - corner[a][c] * corner[a][b]
        for i in range(home, size // 8):
            if i == home and place + PANEL == 8:
                continue
            columns = []
            for b in range(PANEL):
                column = jnp.broadcast_to(tiles[i][:, j + b : j + b + 1], wide)
                for a in range(b):
                    column = column - columns[a] * corner[a][b]
                columns.append(column * scales[b])
            lowered = tiles[i]
            for b in range(PANEL):
                lowered = lowered - columns[b] * rows[b]
            if i == home:
                lowered = jnp.where(sub_id >= place + PANEL, lowered, tiles[i])
            tiles[i] = lowered
        for a in range(PANEL):
            tiles[home] = jnp.where(sub_id == place + a, rows[a], tiles[home])
    work = jnp.concatenate(tiles, axis=0)
    a_ref[...] = block_a
    r_ref[...] = jnp.where(across >= down, work[:, :size], 0.0)
    next_ref[...] = dot(work[:, size:], resid, NN, HIGHEST) * (1.0 / inv_root)


def finish(inv_root, packed, image, probes_t, half):
    size, samples = image.shape
    whole = lambda shape: pl.BlockSpec(shape, lambda i, h: (0,) * len(shape))
    return pl.pallas_call(
        functools.partial(finish_kernel, inv_root),
        grid_spec=pltpu.PrefetchScalarGridSpec(
            num_scalar_prefetch=1,
            grid=(1,),
            in_specs=[
                whole(packed.shape),
                whole(image.shape),
                pl.BlockSpec((size, samples), lambda i, h: (0, h[0])),
            ],
            out_specs=[whole((size, size)), whole((size, size)), whole((size, samples))],
        ),
        out_shape=[
            jax.ShapeDtypeStruct((size, size), jnp.float32),
            jax.ShapeDtypeStruct((size, size), jnp.float32),
            jax.ShapeDtypeStruct((size, samples), jnp.float32),
        ],
        name="finish",
    )(half, packed, image, probes_t)


def ring_sum(value, shift):
    one, two, three = (send(value, shift(s)) for s in (1, 2, 3))
    return (value + two) + (one + three)


def lanczos_step(
    tokens, lengths, embed, conv_w, conv_b, inv_len, hyper, probes, prev_probes, coupling
):
    total_rows = tokens.shape[0] * lax.axis_size("blk")
    inv_root = 1.0 / math.sqrt(total_rows)
    half = lax.axis_index("rep").astype(jnp.int32).reshape(1)
    probes_t = probes.T
    cols, rows = conv_features(
        tokens.T, lengths, embed, conv_w, conv_b, inv_len, probes_t, half
    )
    near = [send(cols, shift_by_core(s, 0)) for s in (1, 2, 3)]
    all_rows = [rows] + [send(rows, shift_y(s)) for s in (1, 2, 3)]
    group = jnp.stack([cols] + near)
    far = [send(group, shift_by_core(s, 1)) for s in (1, 3, 2)]
    swap = core_swap()

    def apply(blocks, start=()):
        return apply_rows(hyper, all_rows, blocks, start)

    partial = apply([group, send(group, swap)])
    partial = apply([far[0], far[1]], [partial])
    swapped = [send(far[0], swap), send(far[1], swap)]
    partial = apply(swapped + [far[2]], [partial])
    partial = apply([send(far[2], swap)], [partial])
    parts = [partial[0]] + [send(partial[s], shift_y(-s)) for s in (1, 2, 3)]
    image, packed = gram_stage(inv_root, hyper, parts, probes_t, prev_probes.T, coupling, half)
    packed = packed + send(packed, core_swap())
    for shift in (shift_z, shift_x, shift_y):
        packed = ring_sum(packed, shift)
    block_a, upper, next_t = finish(inv_root, packed, image, probes_t, half)
    return (block_a, upper, next_t.T)


def solution(mesh):
    return jax.shard_map(
        lanczos_step,
        mesh=mesh,
        in_specs=(
            P("blk", None),
            P("blk"),
            P(),
            P(),
            P(),
            P(),
            P(),
            P("blk", None),
            P(("blk", "rep"), None),
            P(),
        ),
        out_specs=(P(), P(), P(("blk", "rep"), None)),
        check_vma=False,
    )
```

```python
import functools
import math

import jax
import jax.numpy as jnp
from jax import lax
from jax.experimental import pallas as pl
from jax.experimental.pallas import tpu as pltpu
from jax.sharding import PartitionSpec as P


LOG2E = math.log2(math.e)
HIGHEST = lax.Precision.HIGHEST
AXES = ("blk", "rep")
RING = 4


def coords_of(index):
    rep, blk = index % 2, index // 2
    return blk // 16, (blk // 4) % 4, rep * 2 + (blk // 2) % 2, blk % 2


def index_of(z, x, y, core):
    return (((z * 4 + x) * 2 + y % 2) * 2 + core) * 2 + y // 2


def moved(move):
    return [(i, index_of(*move(*coords_of(i)))) for i in range(128)]


def core_swap():
    return moved(lambda z, x, y, c: (z, x, y, 1 - c))


def shift_y(step):
    return moved(lambda z, x, y, c: (z, x, (y + step) % RING, c))


def shift_z(step):
    return moved(lambda z, x, y, c: ((z + step) % RING, x, y, c))


def shift_x(step):
    return moved(lambda z, x, y, c: (z, (x + step) % RING, y, c))


def shift_by_core(step, core_of_z):
    def move(z, x, y, c):
        if c == core_of_z:
            return (z + step) % RING, x, y, c
        return z, (x + step) % RING, y, c

    return moved(move)


def send(value, perm):
    return lax.ppermute(value, AXES, perm)


def dot(left, right, dims, precision=None):
    return lax.dot_general(
        left, right, (dims, ((), ())), precision=precision, preferred_element_type=jnp.float32
    )


NN = ((1,), (0,))
NT = ((1,), (1,))
TN = ((0,), (0,))


CONV_STEP = 4


def conv_kernel(
    taps, half_ref, hyper_ref, tok_ref, len_ref, embed_ref, w_ref, bias_ref, inv_len_ref,
    probe_ref, prev_ref, coupling_ref, cols_ref, rows_ref, known_ref,
    high_ref, low_ref, onehot_ref, acc_ref,
):
    del half_ref
    vocab, channels = embed_ref.shape
    width = w_ref.shape[1]
    seq, samples = tok_ref.shape
    outputs = (seq - taps) // 2 + 1
    depth = high_ref.shape[0]
    lanes = 2 * vocab
    group_in = lax.broadcasted_iota(jnp.int32, (channels, channels), 0) // width
    group_out = lax.broadcasted_iota(jnp.int32, (channels, channels), 1) // width
    same = group_in == group_out
    embed = embed_ref[...]
    high_ref[taps * vocab :, :] = jnp.zeros((depth - taps * vocab, channels), jnp.bfloat16)
    low_ref[taps * vocab :, :] = jnp.zeros((depth - taps * vocab, channels), jnp.bfloat16)
    for k in range(taps):
        tiled = jnp.concatenate([w_ref[k].astype(jnp.float32)] * (channels // width), axis=0)
        dense = jnp.where(same, tiled, 0.0).astype(jnp.bfloat16)
        entry = dot(embed, dense, NN)
        if k == 0:
            entry = entry + bias_ref[...]
        high = entry.astype(jnp.bfloat16)
        high_ref[k * vocab : (k + 1) * vocab, :] = high
        low_ref[k * vocab : (k + 1) * vocab, :] = (
            entry - high.astype(jnp.float32)
        ).astype(jnp.bfloat16)

    known_ref[...] = hyper_ref[1] * probe_ref[...].astype(jnp.float32) - dot(
        coupling_ref[...], prev_ref[...].astype(jnp.float32), NN, HIGHEST
    )

    tokens = jnp.concatenate(
        [tok_ref[...], jnp.full((lanes - seq, samples), -1, jnp.int32)], axis=0
    ).astype(jnp.float32).T
    lane_id = lax.broadcasted_iota(jnp.int32, (samples, lanes), 1)
    left_half = lane_id < vocab
    vocab_id = jnp.where(left_half, lane_id, lane_id - vocab).astype(jnp.float32)
    for s in range(0, seq, 2):
        even = jnp.broadcast_to(tokens[:, s : s + 1], (samples, lanes))
        odd = jnp.broadcast_to(tokens[:, s + 1 : s + 2], (samples, lanes))
        hit = jnp.where(left_half, even, odd) == vocab_id
        onehot_ref[:, s * vocab : (s + 2) * vocab] = jnp.where(hit, 1.0, 0.0).astype(jnp.bfloat16)

    counts_row = (len_ref[...] - taps) // 2 + 1
    counts = jnp.broadcast_to(counts_row.astype(jnp.float32), (lanes, samples)).T
    counts = jnp.concatenate([counts] * (channels // lanes), axis=1)
    acc_ref[...] = jnp.zeros_like(acc_ref)
    root = math.sqrt(2.0 / math.pi)

    def positions(step, carry):
        base = step * CONV_STEP
        window = jnp.concatenate(
            [
                onehot_ref[:, pl.ds(pl.multiple_of((base + q) * lanes, lanes), depth)]
                for q in range(CONV_STEP)
            ],
            axis=0,
        )
        pre = dot(window, high_ref[...], NN) + dot(window, low_ref[...], NN)
        inner = pre * (root + (root * 0.044715) * (pre * pre))
        active = pre + pre * jnp.tanh(inner)
        total = acc_ref[...]
        for q in range(CONV_STEP):
            place = (base + q).astype(jnp.float32)
            part = active[q * samples : (q + 1) * samples, :]
            total = total + jnp.where(place < counts, part, 0.0)
        acc_ref[...] = total
        return carry

    lax.fori_loop(0, outputs // CONV_STEP, positions, 0)

    pooled = acc_ref[...] * (0.5 / counts)
    centered = pooled - jnp.mean(pooled, axis=1, keepdims=True)
    spread_sq = jnp.mean(centered * centered, axis=1, keepdims=True)
    normed = centered * lax.rsqrt(spread_sq + 1e-05)
    feat = (normed * inv_len_ref[...]).astype(jnp.bfloat16)
    cols_ref[:samples, :] = feat
    cols_ref[samples:, :] = probe_ref[...]
    rows_ref[...] = feat.astype(jnp.float32).T.astype(jnp.bfloat16)


def conv_features(
    hyper, tok_t, lengths, embed, conv_w, conv_b, inv_len, probes_t, prev_t, coupling, half
):
    seq, rows = tok_t.shape
    vocab, channels = embed.shape
    taps = conv_w.shape[0]
    samples = rows // 2
    width = probes_t.shape[0]
    depth = -(-taps * vocab // 128) * 128
    whole = lambda shape: pl.BlockSpec(shape, lambda i, h: (0,) * len(shape))
    part = lambda lead: pl.BlockSpec((lead, samples), lambda i, h: (0, h[0]))
    return pl.pallas_call(
        functools.partial(conv_kernel, taps),
        grid_spec=pltpu.PrefetchScalarGridSpec(
            num_scalar_prefetch=1,
            grid=(1,),
            in_specs=[
                pl.BlockSpec(memory_space=pltpu.SMEM),
                part(seq),
                part(1),
                whole((vocab, channels)),
                whole(conv_w.shape),
                whole((1, channels)),
                whole((1, channels)),
                part(width),
                whole((width, samples)),
                whole((width, width)),
            ],
            out_specs=[
                whole((samples + width, channels)),
                whole((channels, samples)),
                whole((width, samples)),
            ],
            scratch_shapes=[
                pltpu.VMEM((depth, channels), jnp.bfloat16),
                pltpu.VMEM((depth, channels), jnp.bfloat16),
                pltpu.VMEM((samples, (seq + 1) * vocab), jnp.bfloat16),
                pltpu.VMEM((samples, channels), jnp.float32),
            ],
        ),
        out_shape=[
            jax.ShapeDtypeStruct((samples + width, channels), jnp.bfloat16),
            jax.ShapeDtypeStruct((channels, samples), jnp.bfloat16),
            jax.ShapeDtypeStruct((width, samples), jnp.float32),
        ],
        name="conv_features",
    )(
        half, hyper, tok_t, lengths.reshape(1, rows), embed, conv_w,
        conv_b.reshape(1, channels), inv_len.reshape(1, channels), probes_t, prev_t, coupling,
    )


def apply_kernel(row_count, col_count, resume, last, hyper_ref, *refs):
    rows = refs[:row_count]
    cols = refs[row_count : row_count + col_count]
    rest = refs[row_count + col_count :]
    start_refs, rest = rest[:resume], rest[resume:]
    known_refs, out_refs, half_ref = rest[:last], rest[last:-1], rest[-1]
    totals = list(out_refs) if last else [out_refs[0].at[i] for i in range(row_count)]
    depth, _, _ = cols[0].shape
    samples = rows[0].shape[1]
    top = jnp.log2(jnp.full((1, 128), hyper_ref[0], jnp.float32))[:, :1]
    for i in range(row_count):
        total = start_refs[0][i] if resume else jnp.zeros(totals[i].shape, jnp.float32)
        totals[i][...] = total + known_refs[0][...] if last and i == 0 else total
        wide = rows[i][...].astype(jnp.float32)
        half_ref[i : i + 1, :] = (0.5 * LOG2E) * jnp.sum(wide * wide, axis=0, keepdims=True)
    for g in range(col_count):
        feat = jnp.concatenate([cols[g][d, :samples, :] for d in range(depth)], axis=0)
        probes = jnp.concatenate([cols[g][d, samples:, :] for d in range(depth)], axis=1)
        wide = feat.astype(jnp.float32)
        bias = (0.5 * LOG2E) * jnp.sum(wide * wide, axis=1, keepdims=True) - top
        bias = jnp.broadcast_to(bias, (depth * samples, samples))
        for i in range(row_count):
            inner = dot(feat, rows[i][...], NN)
            power = jnp.minimum(inner * LOG2E - bias - half_ref[i : i + 1, :], top)
            weights = jnp.exp2(power).astype(jnp.bfloat16)
            totals[i][...] += dot(probes, weights, NN)


def apply_rows(hyper, rows, cols, start=(), known=()):
    depth, tall, channels = cols[0].shape
    samples = rows[0].shape[1]
    width = tall - samples
    last = len(known)
    vmem = pl.BlockSpec(memory_space=pltpu.VMEM)
    pairs = len(cols) * depth * len(rows) * samples * samples
    shape = (len(rows), width, samples)
    return pl.pallas_call(
        functools.partial(apply_kernel, len(rows), len(cols), len(start), last),
        out_shape=[jax.ShapeDtypeStruct(shape[1:], jnp.float32)] * len(rows)
        if last
        else jax.ShapeDtypeStruct(shape, jnp.float32),
        in_specs=[pl.BlockSpec(memory_space=pltpu.SMEM)]
        + [vmem] * (len(rows) + len(cols) + len(start) + last),
        out_specs=[vmem] * len(rows) if last else vmem,
        scratch_shapes=[pltpu.VMEM((len(rows), samples), jnp.float32)],
        compiler_params=pltpu.CompilerParams(vmem_limit_bytes=24 << 20),
        cost_estimate=pl.CostEstimate(
            flops=2 * pairs * (channels + width), transcendentals=pairs, bytes_accessed=4 << 20
        ),
        name="apply_rows",
    )(hyper, *rows, *cols, *start, *known)


def gram_kernel(inv_root, own_ref, one_ref, two_ref, three_ref, col_ref, image_ref, packed_ref):
    size, samples = own_ref.shape
    image = ring_add([own_ref[...], one_ref[...], two_ref[...], three_ref[...]]) * inv_root
    image_ref[...] = image
    probes = col_ref[samples:, :]
    basis_sq = dot(probes, probes, NT) * (inv_root * inv_root)
    rest, projected = image, 0.0
    for _ in range(3):
        piece = rest.astype(jnp.bfloat16)
        rest = rest - piece.astype(jnp.float32)
        projected = projected + dot(probes, piece, NT)
    image_sq = dot(image, image, NT, HIGHEST)
    down = lax.broadcasted_iota(jnp.int32, (size, size), 0)
    across = lax.broadcasted_iota(jnp.int32, (size, size), 1)
    packed_ref[:size, :size] = projected * inv_root
    packed_ref[:size, size:] = jnp.where(across >= down, image_sq, basis_sq)
    diagonal = jnp.sum(jnp.where(across == down, basis_sq, 0.0), axis=0, keepdims=True)
    packed_ref[size:, :size] = jnp.broadcast_to(diagonal, (8, size))
    packed_ref[size:, size:] = jnp.zeros((8, size), jnp.float32)


def gram_stage(inv_root, parts, cols):
    size, samples = parts[0].shape
    vmem = pl.BlockSpec(memory_space=pltpu.VMEM)
    return pl.pallas_call(
        functools.partial(gram_kernel, inv_root),
        in_specs=[vmem] * (len(parts) + 1),
        out_specs=[vmem, vmem],
        out_shape=[
            jax.ShapeDtypeStruct((size, samples), jnp.float32),
            jax.ShapeDtypeStruct((size + 8, 2 * size), jnp.float32),
        ],
        name="gram_stage",
    )(*parts, cols)


PANEL = 4


def finish_kernel(
    inv_root, half_ref, own_ref, one_ref, two_ref, three_ref, image_ref, probe_ref,
    a_ref, r_ref, next_ref,
):
    size = image_ref.shape[0]
    packed = ring_add([own_ref[...], one_ref[...], two_ref[...], three_ref[...]])
    block_a = packed[:size, :size]
    mixed = packed[:size, size:]
    mixed_t = mixed.T
    diagonal = packed[size : size + 1, :size]
    down = lax.broadcasted_iota(jnp.int32, (size, size), 0)
    across = lax.broadcasted_iota(jnp.int32, (size, size), 1)
    image_sq = jnp.where(across >= down, mixed, mixed_t)
    square = jnp.where(across == down, diagonal, jnp.where(across < down, mixed, mixed_t))
    twice = 2.0 * block_a - dot(square, block_a, NN, HIGHEST)
    gram = image_sq - dot(block_a, twice, TN, HIGHEST)
    basis = probe_ref[...].astype(jnp.float32) * inv_root
    resid = image_ref[...] - dot(block_a, basis, TN, HIGHEST)

    unit = jnp.where(across == down, 1.0, 0.0)
    work = jnp.concatenate([gram, unit], axis=1)
    tiles = [work[8 * i : 8 * i + 8, :] for i in range(size // 8)]
    wide = (8, 2 * size)
    sub_id = lax.broadcasted_iota(jnp.int32, wide, 0)
    for j in range(0, size, PANEL):
        home, place = divmod(j, 8)
        rows = [
            jnp.broadcast_to(tiles[home][place + a : place + a + 1, :], wide)
            for a in range(PANEL)
        ]
        corner = [
            [jnp.broadcast_to(rows[a][:, j + b : j + b + 1], wide) if b >= a else None
             for b in range(PANEL)]
            for a in range(PANEL)
        ]
        scales = []
        for a in range(PANEL):
            scale = lax.rsqrt(corner[a][a])
            scales.append(scale)
            rows[a] = rows[a] * scale
            for b in range(a + 1, PANEL):
                corner[a][b] = corner[a][b] * scale
            for c in range(a + 1, PANEL):
                rows[c] = rows[c] - corner[a][c] * rows[a]
                for b in range(c, PANEL):
                    corner[c][b] = corner[c][b] - corner[a][c] * corner[a][b]
        for i in range(home, size // 8):
            if i == home and place + PANEL == 8:
                continue
            columns = []
            for b in range(PANEL):
                column = jnp.broadcast_to(tiles[i][:, j + b : j + b + 1], wide)
                for a in range(b):
                    column = column - columns[a] * corner[a][b]
                columns.append(column * scales[b])
            lowered = tiles[i]
            for b in range(PANEL):
                lowered = lowered - columns[b] * rows[b]
            if i == home:
                lowered = jnp.where(sub_id >= place + PANEL, lowered, tiles[i])
            tiles[i] = lowered
        for a in range(PANEL):
            tiles[home] = jnp.where(sub_id == place + a, rows[a], tiles[home])
    work = jnp.concatenate(tiles, axis=0)
    a_ref[...] = block_a
    r_ref[...] = jnp.where(across >= down, work[:, :size], 0.0)
    next_ref[...] = dot(work[:, size:], resid, NN, HIGHEST) * (1.0 / inv_root)


def finish(inv_root, packed, image, probes_t, half):
    size, samples = image.shape
    whole = lambda shape: pl.BlockSpec(shape, lambda i, h: (0,) * len(shape))
    return pl.pallas_call(
        functools.partial(finish_kernel, inv_root),
        grid_spec=pltpu.PrefetchScalarGridSpec(
            num_scalar_prefetch=1,
            grid=(1,),
            in_specs=[
                *[whole(part.shape) for part in packed],
                whole(image.shape),
                pl.BlockSpec((size, samples), lambda i, h: (0, h[0])),
            ],
            out_specs=[whole((size, size)), whole((size, size)), whole((size, samples))],
        ),
        out_shape=[
            jax.ShapeDtypeStruct((size, size), jnp.float32),
            jax.ShapeDtypeStruct((size, size), jnp.float32),
            jax.ShapeDtypeStruct((size, samples), jnp.float32),
        ],
        name="finish",
    )(half, *packed, image, probes_t)


def ring_parts(value, shift):
    return [value] + [send(value, shift(s)) for s in (1, 2, 3)]


def ring_add(parts):
    return (parts[0] + parts[2]) + (parts[1] + parts[3])


def lanczos_step(
    tokens, lengths, embed, conv_w, conv_b, inv_len, hyper, probes, prev_probes, coupling
):
    total_rows = tokens.shape[0] * lax.axis_size("blk")
    inv_root = 1.0 / math.sqrt(total_rows)
    half = lax.axis_index("rep").astype(jnp.int32).reshape(1)
    probes_t = probes.T
    cols, rows, known = conv_features(
        hyper, tokens.T, lengths, embed, conv_w, conv_b, inv_len, probes_t, prev_probes.T,
        coupling, half,
    )
    near = [send(cols, shift_by_core(s, 0)) for s in (1, 2, 3)]
    all_rows = [rows] + [send(rows, shift_y(s)) for s in (1, 2, 3)]
    group = jnp.stack([cols] + near)
    far = [send(group, shift_by_core(s, 1)) for s in (1, 3, 2)]
    swap = core_swap()

    def apply(blocks, start=(), known=()):
        return apply_rows(hyper, all_rows, blocks, start, known)

    partial = apply([group])
    partial = apply([send(group, swap)], [partial])
    partial = apply([far[0]], [partial])
    partial = apply([send(far[0], swap)], [partial])
    partial = apply([far[1]], [partial])
    partial = apply([send(far[1], swap)], [partial])
    partial = apply([far[2]], [partial])
    partial = apply([send(far[2], swap)], [partial], [known])
    parts = [partial[0]] + [send(partial[s], shift_y(-s)) for s in (1, 2, 3)]
    image, packed = gram_stage(inv_root, parts, cols)
    packed = packed + send(packed, core_swap())
    packed = ring_add(ring_parts(packed, shift_z))
    packed = ring_add(ring_parts(packed, shift_x))
    packed = ring_parts(packed, shift_y)
    block_a, upper, next_t = finish(inv_root, packed, image, probes_t, half)
    return (block_a, upper, next_t.T)


def solution(mesh):
    return jax.shard_map(
        lanczos_step,
        mesh=mesh,
        in_specs=(
            P("blk", None),
            P("blk"),
            P(),
            P(),
            P(),
            P(),
            P(),
            P("blk", None),
            P(("blk", "rep"), None),
            P(),
        ),
        out_specs=(P(), P(), P(("blk", "rep"), None)),
        check_vma=False,
    )
```

```python
import functools
import math

import jax
import jax.numpy as jnp
from jax import lax
from jax.experimental import pallas as pl
from jax.experimental.pallas import tpu as pltpu
from jax.sharding import PartitionSpec as P


LOG2E = math.log2(math.e)
HIGHEST = lax.Precision.HIGHEST
AXES = ("blk", "rep")
RING = 4


def coords_of(index):
    rep, blk = index % 2, index // 2
    return blk // 16, (blk // 4) % 4, rep * 2 + (blk // 2) % 2, blk % 2


def index_of(z, x, y, core):
    return (((z * 4 + x) * 2 + y % 2) * 2 + core) * 2 + y // 2


def moved(move):
    return [(i, index_of(*move(*coords_of(i)))) for i in range(128)]


def core_swap():
    return moved(lambda z, x, y, c: (z, x, y, 1 - c))


def shift_y(step):
    return moved(lambda z, x, y, c: (z, x, (y + step) % RING, c))


def shift_z(step):
    return moved(lambda z, x, y, c: ((z + step) % RING, x, y, c))


def shift_x(step):
    return moved(lambda z, x, y, c: (z, (x + step) % RING, y, c))


def shift_by_core(step, core_of_z):
    def move(z, x, y, c):
        if c == core_of_z:
            return (z + step) % RING, x, y, c
        return z, (x + step) % RING, y, c

    return moved(move)


def send(value, perm):
    return lax.ppermute(value, AXES, perm)


def dot(left, right, dims, precision=None):
    return lax.dot_general(
        left, right, (dims, ((), ())), precision=precision, preferred_element_type=jnp.float32
    )


NN = ((1,), (0,))
NT = ((1,), (1,))
TN = ((0,), (0,))


CONV_STEP = 4
ONEHOT_TYPE = jnp.bfloat16


def conv_kernel(
    taps, half_ref, hyper_ref, tok_ref, len_ref, embed_ref, w_ref, bias_ref, inv_len_ref,
    probe_ref, prev_ref, coupling_ref, cols_ref, rows_ref, known_ref,
    table_ref, onehot_ref, acc_ref,
):
    del half_ref
    vocab, channels = embed_ref.shape
    width = w_ref.shape[1]
    seq, samples = tok_ref.shape
    outputs = (seq - taps) // 2 + 1
    depth = table_ref.shape[0] // 2
    lanes = 2 * vocab
    group_in = lax.broadcasted_iota(jnp.int32, (channels, channels), 0) // width
    group_out = lax.broadcasted_iota(jnp.int32, (channels, channels), 1) // width
    same = group_in == group_out
    embed = embed_ref[...]
    for base in (0, depth):
        table_ref[base + taps * vocab : base + depth, :] = jnp.zeros(
            (depth - taps * vocab, channels), jnp.bfloat16
        )
    for k in range(taps):
        tiled = jnp.concatenate([w_ref[k].astype(jnp.float32)] * (channels // width), axis=0)
        dense = jnp.where(same, tiled, 0.0).astype(jnp.bfloat16)
        entry = dot(embed, dense, NN)
        if k == 0:
            entry = entry + bias_ref[...]
        high = entry.astype(jnp.bfloat16)
        low = (entry - high.astype(jnp.float32)).astype(jnp.bfloat16)
        table_ref[k * vocab : (k + 1) * vocab, :] = high
        table_ref[depth + k * vocab : depth + (k + 1) * vocab, :] = low

    known_ref[...] = hyper_ref[1] * probe_ref[...].astype(jnp.float32) - dot(
        coupling_ref[...], prev_ref[...].astype(jnp.float32), NN, HIGHEST
    )

    vocab_id = lax.broadcasted_iota(jnp.int32, (vocab, samples), 0)

    def hits(s):
        if s >= seq:
            return jnp.zeros((vocab, samples), ONEHOT_TYPE)
        hit = jnp.broadcast_to(tok_ref[s : s + 1, :], (vocab, samples)) == vocab_id
        return jnp.where(hit, 1.0, 0.0).astype(ONEHOT_TYPE)

    for s in range(0, seq, 2):
        pair = jnp.concatenate([hits(s), hits(s + 1)], axis=0)
        onehot_ref[:, s * vocab : (s + 2) * vocab] = pair.T.astype(jnp.bfloat16)

    counts_row = (len_ref[...] - taps) // 2 + 1
    counts = jnp.broadcast_to(counts_row.astype(jnp.float32), (lanes, samples)).T
    counts = jnp.concatenate([counts] * (channels // lanes), axis=1)
    acc_ref[...] = jnp.zeros_like(acc_ref)
    root = math.sqrt(2.0 / math.pi)

    def positions(step, carry):
        base = step * CONV_STEP
        window = jnp.concatenate(
            [
                onehot_ref[:, pl.ds(pl.multiple_of((base + q) * lanes, lanes), depth)]
                for q in range(CONV_STEP)
            ],
            axis=0,
        )
        pre = dot(jnp.concatenate([window, window], axis=1), table_ref[...], NN)
        inner = pre * (root + (root * 0.044715) * (pre * pre))
        active = pre + pre * jnp.tanh(inner)
        total = acc_ref[...]
        for q in range(CONV_STEP):
            place = (base + q).astype(jnp.float32)
            part = active[q * samples : (q + 1) * samples, :]
            total = total + jnp.where(place < counts, part, 0.0)
        acc_ref[...] = total
        return carry

    lax.fori_loop(0, outputs // CONV_STEP, positions, 0)

    pooled = acc_ref[...] * (0.5 / counts)
    centered = pooled - jnp.mean(pooled, axis=1, keepdims=True)
    spread_sq = jnp.mean(centered * centered, axis=1, keepdims=True)
    normed = centered * lax.rsqrt(spread_sq + 1e-05)
    feat = (normed * inv_len_ref[...]).astype(jnp.bfloat16)
    cols_ref[:samples, :] = feat
    cols_ref[samples:, :] = probe_ref[...]
    rows_ref[...] = feat.astype(jnp.float32).T.astype(jnp.bfloat16)


def conv_features(
    hyper, tok_t, lengths, embed, conv_w, conv_b, inv_len, probes_t, prev_t, coupling, half
):
    seq, rows = tok_t.shape
    vocab, channels = embed.shape
    taps = conv_w.shape[0]
    samples = rows // 2
    width = probes_t.shape[0]
    depth = -(-taps * vocab // 128) * 128
    whole = lambda shape: pl.BlockSpec(shape, lambda i, h: (0,) * len(shape))
    part = lambda lead: pl.BlockSpec((lead, samples), lambda i, h: (0, h[0]))
    return pl.pallas_call(
        functools.partial(conv_kernel, taps),
        grid_spec=pltpu.PrefetchScalarGridSpec(
            num_scalar_prefetch=1,
            grid=(1,),
            in_specs=[
                pl.BlockSpec(memory_space=pltpu.SMEM),
                part(seq),
                part(1),
                whole((vocab, channels)),
                whole(conv_w.shape),
                whole((1, channels)),
                whole((1, channels)),
                part(width),
                whole((width, samples)),
                whole((width, width)),
            ],
            out_specs=[
                whole((samples + width, channels)),
                whole((channels, samples)),
                whole((width, samples)),
            ],
            scratch_shapes=[
                pltpu.VMEM((2 * depth, channels), jnp.bfloat16),
                pltpu.VMEM((samples, (seq + 1) * vocab), jnp.bfloat16),
                pltpu.VMEM((samples, channels), jnp.float32),
            ],
        ),
        out_shape=[
            jax.ShapeDtypeStruct((samples + width, channels), jnp.bfloat16),
            jax.ShapeDtypeStruct((channels, samples), jnp.bfloat16),
            jax.ShapeDtypeStruct((width, samples), jnp.float32),
        ],
        name="conv_features",
    )(
        half, hyper, tok_t, lengths.reshape(1, rows), embed, conv_w,
        conv_b.reshape(1, channels), inv_len.reshape(1, channels), probes_t, prev_t, coupling,
    )


def apply_kernel(row_count, col_count, resume, known_count, hyper_ref, *refs):
    rows, refs = refs[:row_count], refs[row_count:]
    cols, refs = refs[:col_count], refs[col_count:]
    starts, refs = refs[: row_count * resume], refs[row_count * resume :]
    known_refs, refs = refs[:known_count], refs[known_count:]
    totals, half_ref = refs[:row_count], refs[row_count]
    depth, _, _ = cols[0].shape
    samples = rows[0].shape[1]
    top = jnp.log2(jnp.full((1, 128), hyper_ref[0], jnp.float32))[:, :1]
    for i in range(row_count):
        total = starts[i][...] if resume else jnp.zeros(totals[i].shape, jnp.float32)
        totals[i][...] = total + known_refs[0][...] if known_count and i == 0 else total
        wide = rows[i][...].astype(jnp.float32)
        half_ref[i : i + 1, :] = (0.5 * LOG2E) * jnp.sum(wide * wide, axis=0, keepdims=True)
    for g in range(col_count):
        feat = jnp.concatenate([cols[g][d, :samples, :] for d in range(depth)], axis=0)
        probes = jnp.concatenate([cols[g][d, samples:, :] for d in range(depth)], axis=1)
        wide = feat.astype(jnp.float32)
        bias = (0.5 * LOG2E) * jnp.sum(wide * wide, axis=1, keepdims=True) - top
        bias = jnp.broadcast_to(bias, (depth * samples, samples))
        for i in range(row_count):
            inner = dot(feat, rows[i][...], NN)
            power = jnp.minimum(inner * LOG2E - bias - half_ref[i : i + 1, :], top)
            weights = jnp.exp2(power).astype(jnp.bfloat16)
            totals[i][...] += dot(probes, weights, NN)


def apply_rows(hyper, rows, cols, starts=(), known=()):
    depth, tall, channels = cols[0].shape
    samples = rows[0].shape[1]
    width = tall - samples
    vmem = pl.BlockSpec(memory_space=pltpu.VMEM)
    pairs = len(cols) * depth * len(rows) * samples * samples
    return pl.pallas_call(
        functools.partial(apply_kernel, len(rows), len(cols), 1 if starts else 0, len(known)),
        out_shape=[jax.ShapeDtypeStruct((width, samples), jnp.float32)] * len(rows),
        in_specs=[pl.BlockSpec(memory_space=pltpu.SMEM)]
        + [vmem] * (len(rows) + len(cols) + len(starts) + len(known)),
        out_specs=[vmem] * len(rows),
        scratch_shapes=[pltpu.VMEM((8, samples), jnp.float32)],
        compiler_params=pltpu.CompilerParams(vmem_limit_bytes=24 << 20),
        cost_estimate=pl.CostEstimate(
            flops=2 * pairs * (channels + width), transcendentals=pairs, bytes_accessed=4 << 20
        ),
        name="apply_rows",
    )(hyper, *rows, *cols, *starts, *known)


def gram_kernel(inv_root, own_ref, one_ref, two_ref, three_ref, col_ref, image_ref, packed_ref):
    size, samples = own_ref.shape
    image = ring_add([own_ref[...], one_ref[...], two_ref[...], three_ref[...]]) * inv_root
    image_ref[...] = image
    probes = col_ref[samples:, :]
    basis_sq = dot(probes, probes, NT) * (inv_root * inv_root)
    rest, projected = image, 0.0
    for _ in range(3):
        piece = rest.astype(jnp.bfloat16)
        rest = rest - piece.astype(jnp.float32)
        projected = projected + dot(probes, piece, NT)
    image_sq = dot(image, image, NT, HIGHEST)
    down = lax.broadcasted_iota(jnp.int32, (size, size), 0)
    across = lax.broadcasted_iota(jnp.int32, (size, size), 1)
    packed_ref[:size, :size] = projected * inv_root
    packed_ref[:size, size:] = jnp.where(across >= down, image_sq, basis_sq)
    diagonal = jnp.sum(jnp.where(across == down, basis_sq, 0.0), axis=0, keepdims=True)
    packed_ref[size:, :size] = jnp.broadcast_to(diagonal, (8, size))
    packed_ref[size:, size:] = jnp.zeros((8, size), jnp.float32)


def gram_stage(inv_root, parts, cols):
    size, samples = parts[0].shape
    vmem = pl.BlockSpec(memory_space=pltpu.VMEM)
    return pl.pallas_call(
        functools.partial(gram_kernel, inv_root),
        in_specs=[vmem] * (len(parts) + 1),
        out_specs=[vmem, vmem],
        out_shape=[
            jax.ShapeDtypeStruct((size, samples), jnp.float32),
            jax.ShapeDtypeStruct((size + 8, 2 * size), jnp.float32),
        ],
        name="gram_stage",
    )(*parts, cols)


PANEL = 8


def finish_kernel(
    inv_root, half_ref, own_ref, one_ref, two_ref, three_ref, image_ref, probe_ref,
    a_ref, r_ref, next_ref,
):
    size = image_ref.shape[0]
    packed = ring_add([own_ref[...], one_ref[...], two_ref[...], three_ref[...]])
    block_a = packed[:size, :size]
    mixed = packed[:size, size:]
    mixed_t = mixed.T
    diagonal = packed[size : size + 1, :size]
    down = lax.broadcasted_iota(jnp.int32, (size, size), 0)
    across = lax.broadcasted_iota(jnp.int32, (size, size), 1)
    image_sq = jnp.where(across >= down, mixed, mixed_t)
    square = jnp.where(across == down, diagonal, jnp.where(across < down, mixed, mixed_t))
    twice = 2.0 * block_a - dot(square, block_a, NN, HIGHEST)
    gram = image_sq - dot(block_a, twice, TN, HIGHEST)
    basis = probe_ref[...].astype(jnp.float32) * inv_root
    resid = image_ref[...] - dot(block_a, basis, TN, HIGHEST)

    unit = jnp.where(across == down, 1.0, 0.0)
    work = jnp.concatenate([gram, unit], axis=1)
    tiles = [work[8 * i : 8 * i + 8, :] for i in range(size // 8)]
    wide = (8, 2 * size)
    sub_id = lax.broadcasted_iota(jnp.int32, wide, 0)
    for j in range(0, size, PANEL):
        home, place = divmod(j, 8)
        rows = [
            jnp.broadcast_to(tiles[home][place + a : place + a + 1, :], wide)
            for a in range(PANEL)
        ]
        corner = [
            [jnp.broadcast_to(rows[a][:, j + b : j + b + 1], wide) if b >= a else None
             for b in range(PANEL)]
            for a in range(PANEL)
        ]
        scales = []
        for a in range(PANEL):
            scale = lax.rsqrt(corner[a][a])
            scales.append(scale)
            rows[a] = rows[a] * scale
            for b in range(a + 1, PANEL):
                corner[a][b] = corner[a][b] * scale
            for c in range(a + 1, PANEL):
                rows[c] = rows[c] - corner[a][c] * rows[a]
                for b in range(c, PANEL):
                    corner[c][b] = corner[c][b] - corner[a][c] * corner[a][b]
        for i in range(home, size // 8):
            if i == home and place + PANEL == 8:
                continue
            columns = []
            for b in range(PANEL):
                column = jnp.broadcast_to(tiles[i][:, j + b : j + b + 1], wide)
                for a in range(b):
                    column = column - columns[a] * corner[a][b]
                columns.append(column * scales[b])
            lowered = tiles[i]
            for b in range(PANEL):
                lowered = lowered - columns[b] * rows[b]
            if i == home:
                lowered = jnp.where(sub_id >= place + PANEL, lowered, tiles[i])
            tiles[i] = lowered
        for a in range(PANEL):
            tiles[home] = jnp.where(sub_id == place + a, rows[a], tiles[home])
    work = jnp.concatenate(tiles, axis=0)
    a_ref[...] = block_a
    r_ref[...] = jnp.where(across >= down, work[:, :size], 0.0)
    next_ref[...] = dot(work[:, size:], resid, NN, HIGHEST) * (1.0 / inv_root)


def finish(inv_root, packed, image, probes_t, half):
    size, samples = image.shape
    whole = lambda shape: pl.BlockSpec(shape, lambda i, h: (0,) * len(shape))
    return pl.pallas_call(
        functools.partial(finish_kernel, inv_root),
        grid_spec=pltpu.PrefetchScalarGridSpec(
            num_scalar_prefetch=1,
            grid=(1,),
            in_specs=[
                *[whole(part.shape) for part in packed],
                whole(image.shape),
                pl.BlockSpec((size, samples), lambda i, h: (0, h[0])),
            ],
            out_specs=[whole((size, size)), whole((size, size)), whole((size, samples))],
        ),
        out_shape=[
            jax.ShapeDtypeStruct((size, size), jnp.float32),
            jax.ShapeDtypeStruct((size, size), jnp.float32),
            jax.ShapeDtypeStruct((size, samples), jnp.float32),
        ],
        name="finish",
    )(half, *packed, image, probes_t)


def ring_parts(value, shift):
    return [value] + [send(value, shift(s)) for s in (1, 2, 3)]


def ring_add(parts):
    return (parts[0] + parts[2]) + (parts[1] + parts[3])


def lanczos_step(
    tokens, lengths, embed, conv_w, conv_b, inv_len, hyper, probes, prev_probes, coupling
):
    total_rows = tokens.shape[0] * lax.axis_size("blk")
    inv_root = 1.0 / math.sqrt(total_rows)
    half = lax.axis_index("rep").astype(jnp.int32).reshape(1)
    probes_t = probes.T
    cols, rows, known = conv_features(
        hyper, tokens.T, lengths, embed, conv_w, conv_b, inv_len, probes_t, prev_probes.T,
        coupling, half,
    )
    near = [send(cols, shift_by_core(s, 0)) for s in (1, 2, 3)]
    all_rows = [rows] + [send(rows, shift_y(s)) for s in (1, 2, 3)]
    group = jnp.stack([cols] + near)
    far = [send(group, shift_by_core(s, 1)) for s in (1, 3)]
    far.append(send(far[0], shift_by_core(1, 1)))
    swap = core_swap()

    def apply(at, blocks, starts=(), known=()):
        return apply_rows(hyper, all_rows[at], blocks, starts, known)

    own, others = slice(0, 1), slice(1, RING)
    sums = apply(slice(0, RING), [group, send(group, swap)])
    own_sum, sums = sums[:1], sums[1:]
    plus, minus, opposite = far
    sums = apply(others, [plus], sums)
    plus_swapped = send(plus, swap)
    sums = apply(others, [plus_swapped, minus], sums)
    minus_swapped = send(minus, swap)
    sums = apply(others, [minus_swapped], sums)
    own_sum = apply(own, [plus, plus_swapped], own_sum)
    sums = apply(others, [opposite], sums)
    opposite_swapped = send(opposite, swap)
    sums = apply(others, [opposite_swapped], sums)
    parts = [send(sums[s - 1], shift_y(-s)) for s in (1, 2, 3)]
    late = [minus, minus_swapped, opposite, opposite_swapped]
    parts = list(apply(own, late, own_sum, [known])) + parts
    image, packed = gram_stage(inv_root, parts, cols)
    packed = packed + send(packed, core_swap())
    packed = ring_add(ring_parts(packed, shift_z))
    packed = ring_add(ring_parts(packed, shift_x))
    packed = ring_parts(packed, shift_y)
    block_a, upper, next_t = finish(inv_root, packed, image, probes_t, half)
    return (block_a, upper, next_t.T)


def solution(mesh):
    return jax.shard_map(
        lanczos_step,
        mesh=mesh,
        in_specs=(
            P("blk", None),
            P("blk"),
            P(),
            P(),
            P(),
            P(),
            P(),
            P("blk", None),
            P(("blk", "rep"), None),
            P(),
        ),
        out_specs=(P(), P(), P(("blk", "rep"), None)),
        check_vma=False,
    )
```
